32 devices in a mesh: layer: 2 (over y), neuron: 4 (over z), token: 4 (over x, core).
Axes of the slice: x: 2, y: 2, z: 4, core: 2. Of those that a mesh axis runs over, the one named last changes fastest.
Arguments:
- tokens: bfloat16 [4096, 8192], P(('layer', 'token'), 'neuron'), parts along dimension 0, may hold values from -6 to 6
- up_weight: bfloat16 [16384, 14336], P(('layer', 'token'), 'neuron'), parts along dimension 0, may hold values from -0.0625 to 0.0625
- encoder: bfloat16 [16384, 1024], P(('layer', 'token'), 'neuron'), parts along dimension 0, may hold values from -0.0625 to 0.0625
- decoder: bfloat16 [2048, 14336], P(('layer', 'token'), 'neuron'), parts along dimension 0, may hold values from -0.1875 to 0.1875
Outputs:
- grad_encoder: float32 [16384, 1024], P(('layer', 'token'), 'neuron'), parts along dimension 0
- grad_decoder: float32 [2048, 14336], P(('layer', 'token'), 'neuron'), parts along dimension 0
The draws below stay inside these ranges and needn't reach their ends.
There are 2 independent parts, one for each index of `layer`. The reference program is written for one: setup_inputs(seed, part) draws one part's arguments, and reference() takes and returns one part's arrays. A program takes and returns all parts, laid end to end along the dimension named above; each array names one. Nothing has to cross between parts.
All inputs are finite; a program needn't handle non-finite values.
Results may differ from the reference program's by a relative error of at most 0.0034.
Values may be sent and summed in bfloat16 or wider, within the bound.
No kernel may reach another device: no remote copies, remote signals or barrier semaphores. Data moves between devices by JAX's collectives and lax.ppermute only.
A program may use at most 128 MiB of HBM per device.

```python
import math
import jax
import jax.numpy as jnp

D = 8192
FF = 14336
RANK = 1024
TOKENS = 2048


def level_of(stream_key, shape, cuts, least, top_value):
    def one(axis_at, parts):
        steps = jax.random.uniform(jax.random.fold_in(jax.random.fold_in(stream_key, 6), axis_at), (parts,), jnp.float32, least / len(cuts), top_value / len(cuts))
        return jnp.repeat(jnp.exp(steps), shape[axis_at] // parts).reshape((-1,) + (1,) * (len(shape) - axis_at - 1))

    factor_of = one(*cuts[0])
    for cut in cuts[1:]:
        factor_of = factor_of * one(*cut)
    return factor_of


def noise(rng, dims, width, bound, shards=(), kind=jnp.bfloat16):
    loudness = level_of(rng, dims, shards, -0.22, 0.18) if shards else 1.0
    drawn = jax.random.normal(rng, dims, jnp.float32) * width * loudness
    return jnp.minimum(jnp.maximum(drawn, -bound), bound).astype(kind)


def setup_inputs(seed: int = 0, part: int = 0) -> dict:
    keys = jax.random.split(jax.random.key(seed), 5)
    own_keys = jax.random.split(jax.random.fold_in(keys[4], part), 5)
    return {
        "tokens": noise(own_keys[0], (TOKENS, D), 1.0, 6.0, ((0, 4), (1, 4))),
        "up_weight": noise(own_keys[1], (D, FF), D ** -0.5, 0.0625, ((0, 4), (1, 4))),
        "encoder": noise(own_keys[2], (D, RANK), D ** -0.5, 0.0625, ((0, 4), (1, 4))),
        "decoder": noise(own_keys[3], (RANK, FF), RANK ** -0.5, 0.1875, ((0, 4), (1, 4))),
    }


def reference(tokens, up_weight, encoder, decoder):
    labels = jax.nn.relu(jnp.dot(tokens, up_weight, preferred_element_type=jnp.float32))
    hidden = jnp.dot(tokens, encoder, preferred_element_type=jnp.float32).astype(jnp.bfloat16)
    predicted = jnp.dot(hidden, decoder, preferred_element_type=jnp.float32)
    scaled = ((predicted - labels) / math.sqrt(TOKENS)).astype(jnp.bfloat16)
    grad_decoder = jnp.dot(hidden.T, scaled, preferred_element_type=jnp.float32)
    back = jnp.dot(scaled, decoder.T, preferred_element_type=jnp.float32).astype(jnp.bfloat16)
    grad_encoder = jnp.dot(tokens.T, back, preferred_element_type=jnp.float32)
    return (grad_encoder, grad_decoder)
```

```python
import math

import jax
import jax.numpy as jnp
from jax import lax
from jax.sharding import PartitionSpec as P


CHUNKS = 4
F32 = jnp.float32
BF16 = jnp.bfloat16


def dot(left, right, dims=((1,), (0,))):
    return lax.dot_general(left, right, (dims, ((), ())), preferred_element_type=F32)


def pick(array, index, axis=0):
    return lax.dynamic_index_in_dim(array, index, axis, keepdims=False)


def per_device(tokens, up_weight, encoder, decoder):
    row_count, width = tokens.shape
    tokens_on, neurons_on = lax.axis_size("token"), lax.axis_size("neuron")
    cores = 2 if tokens_on % 2 == 0 else 1
    chips = tokens_on // cores
    total_rows = row_count * tokens_on
    me = lax.axis_index("token")
    plane = lax.axis_index("neuron")
    chip, core = me // cores, me % cores
    columns = up_weight.shape[1] // tokens_on
    ranks = encoder.shape[1]

    def swap(array):
        return lax.ppermute(array, "token", [(i, i ^ 1) for i in range(tokens_on)])

    def across(array, step):
        return lax.ppermute(
            array,
            "token",
            [(i, (i // cores + step) % chips * cores + i % cores) for i in range(tokens_on)],
        )

    def upward(array, step):
        return lax.ppermute(
            array, "neuron", [(i, (i + step) % neurons_on) for i in range(neurons_on)]
        )

    def spread_of(rows):
        if neurons_on % tokens_on == 0:
            ratio = neurons_on // tokens_on
            gathered = lax.all_gather(rows, "neuron", axis=0)
            moved = lax.all_to_all(gathered, "token", split_axis=0, concat_axis=0, tiled=True)
            if ratio == 1:
                return moved.reshape(-1, width)
            moved = moved.reshape(tokens_on, ratio, -1, width)
            return moved.transpose(0, 2, 1, 3).reshape(-1, ratio * width)
        gathered = lax.all_gather(rows, "neuron", axis=1, tiled=True)
        return lax.all_to_all(gathered, "token", split_axis=1, concat_axis=0, tiled=True)

    def column_block(step, other):
        at = ((chip + step) % chips) * cores + (core ^ other if cores == 2 else 0)
        return lax.dynamic_slice_in_dim(up_weight, at * columns, columns, 1)

    part = row_count // CHUNKS
    pieces = [spread_of(tokens[k * part : (k + 1) * part]) for k in range(CHUNKS)]
    weights = {
        (step, other): column_block(step, other) for step in range(chips) for other in range(cores)
    }
    decoder_own = lax.all_to_all(
        decoder.reshape(-1, tokens_on, columns), "token", split_axis=1, concat_axis=0
    )
    decoder_own = decoder_own.reshape(-1, columns)

    def labels_of(piece):
        received = None
        for step in list(range(1, chips)) + [0]:
            summed = dot(piece, weights[step, 0])
            if cores == 2:
                summed = summed + swap(dot(piece, weights[step, 1]).astype(BF16)).astype(F32)
            if step:
                moved = across(summed.astype(BF16), step).astype(F32)
                received = moved if received is None else received + moved
        return summed if received is None else summed + received

    def hidden_of(piece):
        terms = dot(piece, encoder).reshape(chips, cores, part, ranks)
        summed = pick(terms, core, 1)
        if cores == 2:
            summed = summed + swap(pick(terms, 1 - core, 1))
        own = pick(summed, chip)
        for step in range(1, chips):
            own = own + across(pick(summed, (chip + step) % chips), step)
        own = own.astype(BF16)
        shared = jnp.zeros((chips, part, ranks), BF16)
        shared = lax.dynamic_update_index_in_dim(shared, own, chip, 0)
        for step in range(1, chips):
            shared = lax.dynamic_update_index_in_dim(
                shared, across(own, step), (chip - step) % chips, 0
            )
        wide = jnp.zeros((neurons_on, chips, part, ranks), BF16)
        wide = lax.dynamic_update_index_in_dim(wide, shared, plane, 0)
        for step in range(1, neurons_on):
            wide = lax.dynamic_update_index_in_dim(
                wide, upward(shared, step), (plane - step) % neurons_on, 0
            )
        wide = wide.transpose(1, 2, 0, 3).reshape(chips, part, neurons_on * ranks)
        return both_cores(wide).reshape(tokens_on * part, -1)

    def both_cores(mine):
        if cores == 1:
            return mine[:, None]
        theirs = swap(mine)
        first = jnp.where(core == 0, mine, theirs)
        second = jnp.where(core == 0, theirs, mine)
        return jnp.stack([first, second], axis=1)

    def back_of(scaled):
        terms = dot(scaled, decoder_own, ((1,), (1,)))
        terms = terms.reshape(chips, cores, part, neurons_on, ranks)
        summed = pick(terms, core, 1)
        if cores == 2:
            summed = summed + swap(pick(terms, 1 - core, 1).astype(BF16)).astype(F32)
        own = pick(summed, plane, 2)
        for step in range(1, neurons_on):
            moved = upward(pick(summed, (plane + step) % neurons_on, 2).astype(BF16), step)
            own = own + moved.astype(F32)
        whole = own
        for step in range(1, chips):
            whole = whole + across(own.astype(BF16), step).astype(F32)
        return both_cores(whole.astype(BF16)).reshape(tokens_on * part, ranks)

    hiddens, scaleds = [], []
    grad_encoder = None
    for piece in pieces:
        hidden = hidden_of(piece)
        labels = jax.nn.relu(labels_of(piece))
        predicted = dot(hidden, decoder_own)
        scaled = ((predicted - labels) / math.sqrt(total_rows)).astype(BF16)
        hiddens.append(hidden)
        scaleds.append(scaled)
        term = dot(piece, back_of(scaled), ((0,), (0,)))
        grad_encoder = term if grad_encoder is None else grad_encoder + term
    grad_decoder = None
    for hidden, scaled in zip(hiddens, scaleds):
        term = dot(hidden, scaled, ((0,), (0,)))
        grad_decoder = term if grad_decoder is None else grad_decoder + term
    grad_decoder = lax.all_to_all(
        grad_decoder.astype(BF16).reshape(tokens_on, -1, columns),
        "token",
        split_axis=0,
        concat_axis=0,
        tiled=True,
    )
    grad_decoder = grad_decoder.transpose(1, 0, 2).reshape(-1, tokens_on * columns)
    return (grad_encoder, grad_decoder.astype(F32))


def solution(mesh):
    return jax.shard_map(
        per_device,
        mesh=mesh,
        in_specs=(P(("layer", "token"), "neuron"),) * 4,
        out_specs=(P(("layer", "token"), "neuron"),) * 2,
        check_vma=False,
    )
```

```python
import math

import jax
import jax.numpy as jnp
from jax import lax
from jax.experimental import pallas as pl
from jax.experimental.pallas import tpu as pltpu
from jax.sharding import PartitionSpec as P


SHARES = (6, 10, 10, 6)
CHUNKS = len(SHARES)
F32 = jnp.float32
BF16 = jnp.bfloat16


def dot(left, right, dims=((1,), (0,))):
    return lax.dot_general(left, right, (dims, ((), ())), preferred_element_type=F32)


def block(array, start, size, axis):
    starts = [start if d == axis else 0 for d in range(array.ndim)]
    sizes = [size if d == axis else n for d, n in enumerate(array.shape)]
    return lax.dynamic_slice(array, starts, sizes, allow_negative_indices=False)


def blocks_kernel(order_ref, left_ref, right_ref, out_ref):
    rows = left_ref.shape[0]
    step = rows // 4 if rows % 64 == 0 else rows
    for start in range(0, rows, step):
        at = pl.ds(start, step)
        out_ref[0, at, :] = jnp.dot(
            left_ref[at, :], right_ref[...], preferred_element_type=F32
        ).astype(BF16)


def column_blocks(left, right, order, columns):
    rows, depth = left.shape
    count = order.shape[0]
    return pl.pallas_call(
        blocks_kernel,
        grid_spec=pltpu.PrefetchScalarGridSpec(
            num_scalar_prefetch=1,
            grid=(count,),
            in_specs=[
                pl.BlockSpec((rows, depth), lambda j, order: (0, 0)),
                pl.BlockSpec((depth, columns), lambda j, order: (0, order[j])),
            ],
            out_specs=pl.BlockSpec((1, rows, columns), lambda j, order: (j, 0, 0)),
        ),
        out_shape=jax.ShapeDtypeStruct((count, rows, columns), BF16),
        compiler_params=pltpu.CompilerParams(vmem_limit_bytes=32 << 20),
        cost_estimate=pl.CostEstimate(
            flops=2 * rows * depth * columns * count,
            bytes_accessed=2 * (rows * depth + (depth + rows) * columns * count),
            transcendentals=0,
        ),
    )(order, left, pltpu.with_memory_space_constraint(right, pltpu.HBM))


def per_device(tokens, up_weight, encoder, decoder):
    row_count, width = tokens.shape
    tokens_on, neurons_on = lax.axis_size("token"), lax.axis_size("neuron")
    cores = 2 if tokens_on % 2 == 0 else 1
    chips = tokens_on // cores
    total_rows = row_count * tokens_on
    me = lax.axis_index("token")
    plane = lax.axis_index("neuron")
    chip, core = lax.div(me, cores), lax.rem(me, cores)
    columns = up_weight.shape[1] // tokens_on
    ranks = encoder.shape[1]
    edges = [row_count * sum(SHARES[:k]) // sum(SHARES) for k in range(len(SHARES) + 1)]

    def swap(array):
        return lax.ppermute(array, "token", [(i, i ^ 1) for i in range(tokens_on)])

    def across(array, step):
        return lax.ppermute(
            array,
            "token",
            [(i, (i // cores + step) % chips * cores + i % cores) for i in range(tokens_on)],
        )

    def exchange(array, step, other):
        pairs = [
            (i, (i // cores + step) % chips * cores + (i % cores ^ other))
            for i in range(tokens_on)
        ]
        return lax.ppermute(array, "token", pairs)

    def upward(array, step):
        return lax.ppermute(
            array, "neuron", [(i, (i + step) % neurons_on) for i in range(neurons_on)]
        )

    def gathered_of(k):
        rows = tokens[edges[k] : edges[k + 1]]
        if neurons_on % tokens_on == 0:
            return lax.all_gather(rows, "neuron", axis=0)
        return lax.all_gather(rows, "neuron", axis=1, tiled=True)

    def spread_of(gathered):
        if neurons_on % tokens_on:
            return lax.all_to_all(
                gathered, "token", split_axis=1, concat_axis=0, tiled=True
            )
        moved = lax.all_to_all(gathered, "token", split_axis=0, concat_axis=0, tiled=True)
        ratio = neurons_on // tokens_on
        if ratio == 1:
            return moved.reshape(-1, width)
        moved = moved.reshape(tokens_on, ratio, -1, width)
        return moved.transpose(0, 2, 1, 3).reshape(-1, ratio * width)

    def half(array, index, axis):
        size = array.shape[axis] // cores
        parts = [lax.slice_in_dim(array, j * size, (j + 1) * size, axis=axis) for j in range(cores)]
        return parts[0] if cores == 1 else jnp.where(index == 0, *parts)

    def both_halves(mine):
        if cores == 1:
            return mine
        theirs = swap(mine)
        first = jnp.where(core == 0, mine, theirs)
        second = jnp.where(core == 0, theirs, mine)
        return jnp.concatenate([first, second], axis=0)

    def partials_of(piece):
        steps = list(range(1, chips)) + [0]
        order = [
            lax.rem(chip + step, chips) * cores + (core ^ other)
            for other in reversed(range(cores))
            for step in steps
        ]
        if columns % 128:
            terms = [
                dot(piece, block(up_weight, at * columns, columns, 1)).astype(BF16)
                for at in order
            ]
            return jnp.stack(terms).reshape(cores, chips, -1, columns)
        terms = column_blocks(piece, up_weight, jnp.stack(order), columns)
        return terms.reshape(cores, chips, -1, columns)

    def labels_of(piece):
        terms = partials_of(piece)
        kept = terms[cores - 1]
        if cores == 2:
            moved = swap(terms[0])
            kept = [kept[j].astype(F32) + moved[j].astype(F32) for j in range(chips)]
        total = kept[chips - 1]
        for step in range(1, chips):
            moved = across(kept[step - 1].astype(BF16), step)
            total = total + moved.astype(F32)
        return total

    def hidden_of(piece):
        terms = dot(piece, encoder)
        summed = half(terms, core, 0)
        if cores == 2:
            sent = half(terms, 1 - core, 0)
            sent = swap(sent)
            summed = summed + sent
        whole = summed
        for step in range(1, chips):
            moved = across(summed, step)
            whole = whole + moved
        shared = [whole.astype(BF16)]
        for step in range(1, neurons_on):
            shared.append(upward(shared[0], step))
        wide = [
            lax.select_n(lax.rem(plane + neurons_on - j, neurons_on), *shared)
            for j in range(neurons_on)
        ]
        return both_halves(jnp.concatenate(wide, axis=1))

    def back_of(scaled, decoder_own):
        terms = dot(scaled, decoder_own, ((1,), (1,)))
        summed = half(terms, core, 0)
        if cores == 2:
            sent = half(terms, 1 - core, 0).astype(BF16)
            sent = swap(sent)
            summed = summed + sent.astype(F32)
        parts = [
            lax.slice_in_dim(summed, j * ranks, (j + 1) * ranks, axis=1)
            for j in range(neurons_on)
        ]
        own = lax.select_n(plane, *parts)
        for step in range(1, neurons_on):
            sent = lax.select_n(lax.rem(plane + step, neurons_on), *parts).astype(BF16)
            moved = upward(sent, step)
            own = own + moved.astype(F32)
        whole = own
        for step in range(1, chips):
            sent = own.astype(BF16)
            moved = across(sent, step)
            whole = whole + moved.astype(F32)
        return both_halves(whole.astype(BF16))

    gathered = [gathered_of(k) for k in range(CHUNKS)]
    arrived = []
    for step in range(chips):
        for other in range(cores):
            there = lax.rem(chip + step, chips) * cores + (core ^ other)
            sent = block(decoder, there * columns, columns, 1)
            if step or other:
                sent = exchange(sent, step, other)
            arrived.append(sent)
    decoder_own = []
    for j in range(tokens_on):
        which = lax.rem(chip + chips - j // cores, chips) * cores + (core ^ (j % cores))
        decoder_own.append(lax.select_n(which, *arrived))
    decoder_own = jnp.concatenate(decoder_own, axis=0)
    grad_encoder, grad_decoder = None, None
    for k in range(CHUNKS):
        piece = spread_of(gathered[k])
        labels = jax.nn.relu(labels_of(piece))
        hidden = hidden_of(piece)
        predicted = dot(hidden, decoder_own)
        scaled = ((predicted - labels) / math.sqrt(total_rows)).astype(BF16)
        term = dot(hidden, scaled, ((0,), (0,)))
        grad_decoder = term if grad_decoder is None else lax.optimization_barrier(grad_decoder) + term
        back = back_of(scaled, decoder_own)
        term = dot(piece, back, ((0,), (0,)))
        grad_encoder = term if grad_encoder is None else lax.optimization_barrier(grad_encoder) + term
    grad_decoder = lax.all_to_all(
        grad_decoder.astype(BF16).reshape(tokens_on, -1, columns),
        "token",
        split_axis=0,
        concat_axis=0,
        tiled=True,
    )
    grad_decoder = jnp.concatenate([grad_decoder[j] for j in range(tokens_on)], axis=1)
    return (grad_encoder, grad_decoder.astype(F32))


def solution(mesh):
    return jax.shard_map(
        per_device,
        mesh=mesh,
        in_specs=(P(("layer", "token"), "neuron"),) * 4,
        out_specs=(P(("layer", "token"), "neuron"),) * 2,
        check_vma=False,
    )
```

```python
import math

import jax
import jax.numpy as jnp
from jax import lax
from jax.experimental import pallas as pl
from jax.experimental.pallas import tpu as pltpu
from jax.sharding import PartitionSpec as P


SHARES = (6, 10, 10, 6)
CHUNKS = len(SHARES)
F32 = jnp.float32
BF16 = jnp.bfloat16


def dot(left, right, dims=((1,), (0,))):
    return lax.dot_general(left, right, (dims, ((), ())), preferred_element_type=F32)


def block(array, start, size, axis):
    starts = [start if d == axis else 0 for d in range(array.ndim)]
    sizes = [size if d == axis else n for d, n in enumerate(array.shape)]
    return lax.dynamic_slice(array, starts, sizes, allow_negative_indices=False)


def blocks_kernel(order_ref, left_ref, right_ref, sent_ref, kept_ref):
    rows = left_ref.shape[0]
    step = rows // 2 if rows % 32 == 0 else rows

    def fill(out_ref):
        for start in range(0, rows, step):
            at = pl.ds(start, step)
            out_ref[0, at, :] = jnp.dot(
                left_ref[at, :], right_ref[...], preferred_element_type=F32
            ).astype(BF16)

    first = pl.program_id(0) < pl.num_programs(0) // 2
    pl.when(first)(lambda: fill(sent_ref))
    pl.when(jnp.logical_not(first))(lambda: fill(kept_ref))


def column_blocks(left, right, order, columns):
    rows, depth = left.shape
    count = order.shape[0]
    half = count // 2
    shape = jax.ShapeDtypeStruct((half, rows, columns), BF16)
    return pl.pallas_call(
        blocks_kernel,
        grid_spec=pltpu.PrefetchScalarGridSpec(
            num_scalar_prefetch=1,
            grid=(count,),
            in_specs=[
                pl.BlockSpec((rows, depth), lambda j, order: (0, 0)),
                pl.BlockSpec((depth, columns), lambda j, order: (0, order[j])),
            ],
            out_specs=[
                pl.BlockSpec((1, rows, columns), lambda j, order: (jnp.minimum(j, half - 1), 0, 0)),
                pl.BlockSpec((1, rows, columns), lambda j, order: (jnp.maximum(j - half, 0), 0, 0)),
            ],
        ),
        out_shape=[shape, shape],
        compiler_params=pltpu.CompilerParams(vmem_limit_bytes=32 << 20),
        cost_estimate=pl.CostEstimate(
            flops=2 * rows * depth * columns * count,
            bytes_accessed=2 * (rows * depth + (depth + rows) * columns * count),
            transcendentals=0,
        ),
    )(order, left, pltpu.with_memory_space_constraint(right, pltpu.HBM))


def arrange_kernel(order_ref, *refs):
    *in_refs, out_ref = refs
    core = order_ref[pl.num_programs(0)]
    for at, (first, second) in ((core, in_refs[::2]), (1 - core, in_refs[1::2])):
        out_ref[0, pl.ds(at, 1)] = (first[...] + second[...]).astype(BF16)


def arranged(early, late, order, count):
    rows, columns = early[0].shape[0] // count, early[0].shape[1]
    spec = pl.BlockSpec((1, rows, columns), lambda p, order: (order[p], 0, 0))
    return pl.pallas_call(
        arrange_kernel,
        grid_spec=pltpu.PrefetchScalarGridSpec(
            num_scalar_prefetch=1,
            grid=(count,),
            in_specs=[spec] * 4,
            out_specs=pl.BlockSpec((1, 2, rows, columns), lambda p, order: (p, 0, 0, 0)),
        ),
        out_shape=jax.ShapeDtypeStruct((count, 2, rows, columns), BF16),
        cost_estimate=pl.CostEstimate(
            flops=0, bytes_accessed=20 * count * rows * columns, transcendentals=0
        ),
    )(order, *(one.reshape(count, rows, columns) for one in (*early, *late)))


def per_device(tokens, up_weight, encoder, decoder):
    row_count, width = tokens.shape
    tokens_on, neurons_on = lax.axis_size("token"), lax.axis_size("neuron")
    cores, chips = 2, tokens_on // 2
    total_rows = row_count * tokens_on
    me = lax.axis_index("token")
    plane = lax.axis_index("neuron")
    chip, core = lax.div(me, cores), lax.rem(me, cores)
    columns = up_weight.shape[1] // tokens_on
    ranks = encoder.shape[1]
    split = ranks // cores
    edges = [row_count * sum(SHARES[:k]) // sum(SHARES) for k in range(len(SHARES) + 1)]
    planes = [lax.rem(plane + neurons_on - j, neurons_on) for j in range(neurons_on)]

    def exchange(array, step, other):
        pairs = [
            (i, (i // cores + step) % chips * cores + (i % cores ^ other))
            for i in range(tokens_on)
        ]
        return lax.ppermute(array, "token", pairs)

    def swap(array):
        return exchange(array, 0, 1)

    def across(array, step):
        return exchange(array, step, 0)

    def upward(array, step):
        return lax.ppermute(
            array, "neuron", [(i, (i + step) % neurons_on) for i in range(neurons_on)]
        )

    def cut(array, j):
        return lax.slice_in_dim(array, j * split, (j + 1) * split, axis=1)

    def gathered_of(k):
        rows = tokens[edges[k] : edges[k + 1]]
        if neurons_on % tokens_on == 0:
            return lax.all_gather(rows, "neuron", axis=0)
        return lax.all_gather(rows, "neuron", axis=1, tiled=True)

    def spread_of(gathered):
        if neurons_on % tokens_on:
            return lax.all_to_all(
                gathered, "token", split_axis=1, concat_axis=0, tiled=True
            )
        moved = lax.all_to_all(gathered, "token", split_axis=0, concat_axis=0, tiled=True)
        ratio = neurons_on // tokens_on
        if ratio == 1:
            return moved.reshape(-1, width)
        moved = moved.reshape(tokens_on, ratio, -1, width)
        return moved.transpose(0, 2, 1, 3).reshape(-1, ratio * width)

    def partials_of(piece):
        steps = list(range(1, chips)) + [0]
        order = [
            lax.rem(chip + step, chips) * cores + (core ^ other)
            for other in (1, 0)
            for step in steps
        ]
        if columns % 128 == 0:
            return column_blocks(piece, up_weight, jnp.stack(order), columns)
        terms = [
            dot(piece, block(up_weight, at * columns, columns, 1)).astype(BF16) for at in order
        ]
        return jnp.stack(terms[:chips]), jnp.stack(terms[chips:])

    def labels_of(piece):
        sent, kept = partials_of(piece)
        moved = swap(sent)
        kept = [kept[j].astype(F32) + moved[j].astype(F32) for j in range(chips)]
        total = kept[chips - 1]
        for step in range(1, chips):
            moved = across(kept[step - 1].astype(BF16), step)
            total = total + moved.astype(F32)
        return total

    def hidden_of(piece, encoder_own):
        terms = dot(piece, encoder_own)
        moved = swap(cut(terms, 0))
        summed = cut(terms, 1) + moved
        whole = summed
        for step in range(1, chips):
            moved = across(summed.astype(BF16), step)
            whole = whole + moved.astype(F32)
        shared = [whole.astype(BF16)]
        for step in range(1, neurons_on):
            shared.append(upward(shared[0], step))
        mine = jnp.concatenate(shared, axis=1)
        return mine, swap(mine)

    def back_of(scaled, decoders):
        terms = dot(scaled, decoders[1], ((1,), (1,))).astype(BF16)
        moved = swap(terms)
        terms = dot(scaled, decoders[0], ((1,), (1,)))
        terms = terms + moved.astype(F32)
        own = cut(terms, 0)
        for step in range(1, neurons_on):
            sent = cut(terms, neurons_on - step).astype(BF16)
            moved = upward(sent, step)
            own = own + moved.astype(F32)
        whole = own
        for step in range(1, chips):
            moved = across(own.astype(BF16), step)
            whole = whole + moved.astype(F32)
        mine = whole.astype(BF16)
        theirs = swap(mine)
        return jnp.concatenate([mine, theirs], axis=1)

    gathered = [gathered_of(k) for k in range(CHUNKS)]
    arrived = []
    for step in range(chips):
        for other in range(cores):
            there = lax.rem(chip + step, chips) * cores + (core ^ other)
            sent = block(decoder, there * columns, columns, 1)
            if step or other:
                sent = exchange(sent, step, other)
            arrived.append(sent)
    rows = []
    for j in range(tokens_on):
        which = lax.rem(chip + chips - j // cores, chips) * cores + (core ^ (j % cores))
        rows.append(lax.select_n(which, *arrived))
    rows = jnp.concatenate(rows, axis=0)
    decoders = [
        jnp.concatenate([block(rows, at * ranks + part * split, split, 0) for at in planes], axis=0)
        for part in (core, 1 - core)
    ]
    encoder_own = jnp.concatenate(
        [block(encoder, part * split, split, 1) for part in (1 - core, core)], axis=1
    )
    grad_encoder = None
    for k in range(CHUNKS):
        piece = spread_of(gathered[k])
        labels = jax.nn.relu(labels_of(piece))
        hiddens = hidden_of(piece, encoder_own)
        predicted = dot(hiddens[0], decoders[0]) + dot(hiddens[1], decoders[1])
        scaled = ((predicted - labels) / math.sqrt(total_rows)).astype(BF16)
        terms = [dot(hidden, scaled, ((0,), (0,))) for hidden in hiddens]
        if k == CHUNKS - 1:
            late_terms = terms
        elif k:
            earlier = lax.optimization_barrier(early_terms)
            early_terms = [one + two for one, two in zip(earlier, terms)]
        else:
            early_terms = terms
        back = back_of(scaled, decoders)
        term = dot(piece, back, ((0,), (0,)))
        if grad_encoder is not None:
            term = lax.optimization_barrier(grad_encoder) + term
        grad_encoder = term
    grad_decoder = arranged(early_terms, late_terms, jnp.stack(planes + [core]), neurons_on)
    grad_decoder = lax.all_to_all(
        grad_decoder.reshape(tokens_on, -1, columns),
        "token",
        split_axis=0,
        concat_axis=0,
        tiled=True,
    )
    grad_decoder = jnp.concatenate([grad_decoder[j] for j in range(tokens_on)], axis=1)
    parts = [grad_encoder[:, :split], grad_encoder[:, split:]]
    grad_encoder = jnp.concatenate(
        [jnp.where(core == 0, *parts), jnp.where(core == 0, *parts[::-1])], axis=1
    )
    return (grad_encoder, grad_decoder.astype(F32))


def solution(mesh):
    return jax.shard_map(
        per_device,
        mesh=mesh,
        in_specs=(P(("layer", "token"), "neuron"),) * 4,
        out_specs=(P(("layer", "token"), "neuron"),) * 2,
        check_vma=False,
    )
```

```python
import math

import jax
import jax.numpy as jnp
from jax import lax
from jax.experimental import pallas as pl
from jax.experimental.pallas import tpu as pltpu
from jax.sharding import PartitionSpec as P


SHARES = (5, 9, 10, 8)
CHUNKS = len(SHARES)
F32 = jnp.float32
BF16 = jnp.bfloat16


def dot(left, right, dims=((1,), (0,))):
    return lax.dot_general(left, right, (dims, ((), ())), preferred_element_type=F32)


def block(array, start, size, axis):
    starts = [start if d == axis else 0 for d in range(array.ndim)]
    sizes = [size if d == axis else n for d, n in enumerate(array.shape)]
    return lax.dynamic_slice(array, starts, sizes, allow_negative_indices=False)


def blocks_kernel(order_ref, left_ref, right_ref, sent_ref, kept_ref):
    rows = left_ref.shape[0]
    step = rows // 2 if rows % 32 == 0 else rows
    first = pl.program_id(0) < pl.num_programs(0) // 2

    @pl.loop(0, rows // step)
    def _(turn):
        at = pl.ds(pl.multiple_of(turn * step, step), step)
        terms = jnp.dot(left_ref[at, :], right_ref[...], preferred_element_type=F32).astype(BF16)

        @pl.when(first)
        def _():
            sent_ref[0, at, :] = terms

        @pl.when(jnp.logical_not(first))
        def _():
            kept_ref[0, at, :] = terms


def column_blocks(left, right, order, columns):
    rows, depth = left.shape
    count = order.shape[0]
    half = count // 2
    shape = jax.ShapeDtypeStruct((half, rows, columns), BF16)
    return pl.pallas_call(
        blocks_kernel,
        grid_spec=pltpu.PrefetchScalarGridSpec(
            num_scalar_prefetch=1,
            grid=(count,),
            in_specs=[
                pl.BlockSpec((rows, depth), lambda j, order: (0, 0)),
                pl.BlockSpec((depth, columns), lambda j, order: (0, order[j])),
            ],
            out_specs=[
                pl.BlockSpec((1, rows, columns), lambda j, order: (jnp.minimum(j, half - 1), 0, 0)),
                pl.BlockSpec((1, rows, columns), lambda j, order: (jnp.maximum(j - half, 0), 0, 0)),
            ],
        ),
        out_shape=[shape, shape],
        compiler_params=pltpu.CompilerParams(vmem_limit_bytes=32 << 20),
        cost_estimate=pl.CostEstimate(
            flops=2 * rows * depth * columns * count,
            bytes_accessed=2 * (rows * depth + (depth + rows) * columns * count),
            transcendentals=0,
        ),
    )(order, left, pltpu.with_memory_space_constraint(right, pltpu.HBM))


def arrange_kernel(order_ref, *refs):
    *in_refs, out_ref = refs
    core = order_ref[pl.num_programs(0)]
    for at, (first, second) in ((core, in_refs[::2]), (1 - core, in_refs[1::2])):
        out_ref[0, pl.ds(at, 1)] = (first[...] + second[...]).astype(BF16)


def arranged(early, late, order, count):
    rows, columns = early[0].shape[0] // count, early[0].shape[1]
    spec = pl.BlockSpec((1, rows, columns), lambda p, order: (order[p], 0, 0))
    return pl.pallas_call(
        arrange_kernel,
        grid_spec=pltpu.PrefetchScalarGridSpec(
            num_scalar_prefetch=1,
            grid=(count,),
            in_specs=[spec] * 4,
            out_specs=pl.BlockSpec((1, 2, rows, columns), lambda p, order: (p, 0, 0, 0)),
        ),
        out_shape=jax.ShapeDtypeStruct((count, 2, rows, columns), BF16),
        cost_estimate=pl.CostEstimate(
            flops=0, bytes_accessed=20 * count * rows * columns, transcendentals=0
        ),
    )(order, *(one.reshape(count, rows, columns) for one in (*early, *late)))


def per_device(tokens, up_weight, encoder, decoder):
    row_count, width = tokens.shape
    tokens_on, neurons_on = lax.axis_size("token"), lax.axis_size("neuron")
    cores, chips = 2, tokens_on // 2
    total_rows = row_count * tokens_on
    me = lax.axis_index("token")
    plane = lax.axis_index("neuron")
    chip, core = lax.div(me, cores), lax.rem(me, cores)
    columns = up_weight.shape[1] // tokens_on
    ranks = encoder.shape[1]
    split = ranks // cores
    edges = [row_count * sum(SHARES[:k]) // sum(SHARES) for k in range(len(SHARES) + 1)]
    planes = [lax.rem(plane + neurons_on - j, neurons_on) for j in range(neurons_on)]

    def exchange(array, step, other):
        pairs = [
            (i, (i // cores + step) % chips * cores + (i % cores ^ other))
            for i in range(tokens_on)
        ]
        return lax.ppermute(array, "token", pairs)

    def swap(array):
        return exchange(array, 0, 1)

    def across(array, step):
        return exchange(array, step, 0)

    def upward(array, step):
        return lax.ppermute(
            array, "neuron", [(i, (i + step) % neurons_on) for i in range(neurons_on)]
        )

    def cut(array, j):
        return lax.slice_in_dim(array, j * split, (j + 1) * split, axis=1)

    def gathered_of(k):
        rows = tokens[edges[k] : edges[k + 1]]
        if neurons_on % tokens_on == 0:
            return lax.all_gather(rows, "neuron", axis=0)
        return lax.all_gather(rows, "neuron", axis=1, tiled=True)

    def spread_of(gathered):
        if neurons_on % tokens_on:
            return lax.all_to_all(
                gathered, "token", split_axis=1, concat_axis=0, tiled=True
            )
        moved = lax.all_to_all(gathered, "token", split_axis=0, concat_axis=0, tiled=True)
        ratio = neurons_on // tokens_on
        if ratio == 1:
            return moved.reshape(-1, width)
        moved = moved.reshape(tokens_on, ratio, -1, width)
        return moved.transpose(0, 2, 1, 3).reshape(-1, ratio * width)

    def partials_of(piece):
        steps = list(range(1, chips)) + [0]
        order = [
            lax.rem(chip + step, chips) * cores + (core ^ other)
            for other in (1, 0)
            for step in steps
        ]
        if columns % 128 == 0:
            return column_blocks(piece, up_weight, jnp.stack(order), columns)
        terms = [
            dot(piece, block(up_weight, at * columns, columns, 1)).astype(BF16) for at in order
        ]
        return jnp.stack(terms[:chips]), jnp.stack(terms[chips:])

    def labels_of(piece):
        sent, kept = partials_of(piece)
        moved = swap(sent)
        kept = [kept[j].astype(F32) + moved[j].astype(F32) for j in range(chips)]
        total = kept[chips - 1]
        for step in range(1, chips):
            moved = across(kept[step - 1].astype(BF16), step)
            total = total + moved.astype(F32)
        return total

    def hidden_of(piece, encoder_own):
        terms = dot(piece, encoder_own)
        moved = swap(cut(terms, 0))
        summed = cut(terms, 1) + moved
        whole = summed
        for step in range(1, chips):
            moved = across(summed, step)
            whole = whole + moved
        shared = [whole.astype(BF16)]
        for step in range(1, neurons_on):
            shared.append(upward(shared[0], step))
        mine = jnp.concatenate(shared, axis=1)
        return mine, swap(mine)

    def back_of(scaled, decoders):
        terms = dot(scaled, decoders[1], ((1,), (1,))).astype(BF16)
        moved = swap(terms)
        terms = dot(scaled, decoders[0], ((1,), (1,)))
        terms = terms + moved.astype(F32)
        own = cut(terms, 0)
        for step in range(1, neurons_on):
            sent = cut(terms, neurons_on - step).astype(BF16)
            moved = upward(sent, step)
            own = own + moved.astype(F32)
        whole = own
        for step in range(1, chips):
            moved = across(own.astype(BF16), step)
            whole = whole + moved.astype(F32)
        mine = whole.astype(BF16)
        theirs = swap(mine)
        return jnp.concatenate([mine, theirs], axis=1)

    gathered = [gathered_of(k) for k in range(CHUNKS)]
    arrived = []
    for step in range(chips):
        for other in range(cores):
            there = lax.rem(chip + step, chips) * cores + (core ^ other)
            sent = block(decoder, there * columns, columns, 1)
            if step or other:
                sent = exchange(sent, step, other)
            arrived.append(sent)
    rows = []
    for j in range(tokens_on):
        which = lax.rem(chip + chips - j // cores, chips) * cores + (core ^ (j % cores))
        rows.append(lax.select_n(which, *arrived))
    rows = jnp.concatenate(rows, axis=0)
    decoders = [
        jnp.concatenate([block(rows, at * ranks + part * split, split, 0) for at in planes], axis=0)
        for part in (core, 1 - core)
    ]
    encoder_own = jnp.concatenate(
        [block(encoder, part * split, split, 1) for part in (1 - core, core)], axis=1
    )
    grad_encoder = None
    for k in range(CHUNKS):
        piece = spread_of(gathered[k])
        labels = jax.nn.relu(labels_of(piece))
        hiddens = hidden_of(piece, encoder_own)
        predicted = dot(hiddens[0], decoders[0]) + dot(hiddens[1], decoders[1])
        scaled = ((predicted - labels) / math.sqrt(total_rows)).astype(BF16)
        terms = [dot(hidden, scaled, ((0,), (0,))) for hidden in hiddens]
        if k == CHUNKS - 1:
            late_terms = terms
        elif k:
            earlier = lax.optimization_barrier(early_terms)
            early_terms = [one + two for one, two in zip(earlier, terms)]
        else:
            early_terms = terms
        back = back_of(scaled, decoders)
        term = dot(piece, back, ((0,), (0,)))
        if grad_encoder is not None:
            term = lax.optimization_barrier(grad_encoder) + term
        grad_encoder = term
    grad_decoder = arranged(early_terms, late_terms, jnp.stack(planes + [core]), neurons_on)
    grad_decoder = lax.all_to_all(
        grad_decoder.reshape(tokens_on, -1, columns),
        "token",
        split_axis=0,
        concat_axis=0,
        tiled=True,
    )
    grad_decoder = jnp.concatenate([grad_decoder[j] for j in range(tokens_on)], axis=1)
    parts = [grad_encoder[:, :split], grad_encoder[:, split:]]
    grad_encoder = jnp.concatenate(
        [jnp.where(core == 0, *parts), jnp.where(core == 0, *parts[::-1])], axis=1
    )
    return (grad_encoder, grad_decoder.astype(F32))


def solution(mesh):
    return jax.shard_map(
        per_device,
        mesh=mesh,
        in_specs=(P(("layer", "token"), "neuron"),) * 4,
        out_specs=(P(("layer", "token"), "neuron"),) * 2,
        check_vma=False,
    )
```
